32 devices in a mesh: parts: 2 (over x), ctx: 4 (over z), branch: 4 (over y, core).
Axes of the slice: x: 2, y: 2, z: 4, core: 2. Of those that a mesh axis runs over, the one named last changes fastest.
Arguments:
- prefix_kv: bfloat16 [2, 8192, 1024], P(None, ('parts', 'ctx')), parts along dimension 1
- queries: bfloat16 [512, 8192], P(('parts', 'ctx', 'branch')), parts along dimension 0
- new_kv: bfloat16 [2, 512, 1024], P(None, ('parts', 'ctx', 'branch')), parts along dimension 1, may hold values from -6 to 6
- suffix_kv: bfloat16 [2, 512, 64, 1024], P(None, ('parts', 'ctx', 'branch')), parts along dimension 1, may hold values from -6 to 6
- suffix_len: int32 [512], P(('parts', 'ctx', 'branch')), parts along dimension 0, may hold values from 1 to 64, as said below
- node_kv: bfloat16 [2, 8, 128, 1024], P(None, ('parts', 'branch')), parts along dimension 1, may hold values from -6 to 6
- node_len: int32 [8], P('parts'), parts along dimension 0, may hold values from 1 to 128, as said below
- parent: int32 [8], P('parts'), parts along dimension 0, may hold values from -1 to 2, as said below
- leaf: int32 [512], P(('parts', 'ctx', 'branch')), parts along dimension 0, may hold values from 0 to 3
Outputs:
- context: bfloat16 [512, 8192], P(('parts', 'ctx', 'branch')), parts along dimension 0
The draws below stay inside these ranges and needn't reach their ends.
There are 2 independent parts, one for each index of `parts`. The reference program is written for one: setup_inputs(seed, part) draws one part's arguments, and reference() takes and returns one part's arrays. A program takes and returns all parts, laid end to end along the dimension named above; each array names one. Nothing has to cross between parts.
Inputs may be any that keep to these rules, and one draw needn't show every extreme that they name: `suffix_len`: live tokens stand first in a rollout's suffix; some rollout has all 64. `node_len`: live tokens stand first in a node; some node has all 128. parent[n] is -1 or a node below n; parent[0] is -1.
All inputs are finite; a program needn't handle non-finite values.
Results may differ from the reference program's by a relative error of at most 0.0055.
Values may be sent and summed in bfloat16 or wider, within the bound.
A program may use at most 128 MiB of HBM per device.

```python
import math
import jax
import jax.numpy as jnp
from jax import lax

HEADS = 64
KV_HEADS = 8
HEAD_DIM = 128
R_DEV = 16
NODE_LEN = 128
SUF = 64
QW = 8192
KVW = 1024
PREFIX = 4096
ROLLOUTS = 256
NODES = 4


def draw_prefix_kv(key, part):
    bulk = jax.random.normal(jax.random.fold_in(key, 11), (2, PREFIX, KVW), jnp.float32)
    return bulk.astype(jnp.bfloat16)


def draw_queries(key, part):
    bulk = 2.5 * jax.random.normal(jax.random.fold_in(key, 19), (ROLLOUTS, HEADS, HEAD_DIM), jnp.float32)
    return bulk.reshape(ROLLOUTS, QW).astype(jnp.bfloat16)


def draw_suffix_len(key, part):
    blocks = ROLLOUTS // R_DEV
    caps = jax.random.randint(jax.random.fold_in(key, 31), (blocks, 1), max(SUF // 4, 1), SUF + 1)
    lengths = jax.random.randint(jax.random.fold_in(key, 32), (blocks, R_DEV), 1, caps + 1).reshape(ROLLOUTS)
    spot = jax.random.randint(jax.random.fold_in(key, 33), (), 0, ROLLOUTS)
    return lengths.at[spot].set(SUF).astype(jnp.int32)


def draw_node_len(key, part):
    lengths = jax.random.randint(jax.random.fold_in(key, 41), (NODES,), 1, NODE_LEN + 1)
    spot = jax.random.randint(jax.random.fold_in(key, 42), (), 0, NODES)
    return lengths.at[spot].set(NODE_LEN).astype(jnp.int32)


def draw_parent(key, part):
    upper = jnp.arange(NODES, dtype=jnp.int32)
    drawn = jax.random.randint(jax.random.fold_in(key, 51), (NODES,), -1, upper).astype(jnp.int32)
    drawn = drawn.at[NODES - 1].set(NODES - 2)
    second = (jnp.asarray(part, jnp.int32) % 2 - 1).astype(jnp.int32)
    drawn = drawn.at[1].set(second)
    return drawn.at[0].set(-1).astype(jnp.int32)


def touch_ends(values, key, smallest, largest):
    longest = values.shape.index(max(values.shape))
    spots = []
    for shift in (0, 1):
        where = [jax.random.randint(jax.random.fold_in(key, axis), (), 0, length) for axis, length in enumerate(values.shape)]
        where[longest] = (where[longest] + shift) % values.shape[longest]
        spots.append(tuple(where))
    return values.at[spots[0]].set(smallest).at[spots[1]].set(largest)


def block_scale(key, shape, shards, smallest, top_value):
    loudness, own = 1.0, jax.random.fold_in(key, 6)
    for position, shards_of in shards:
        draws = jnp.exp(jax.random.uniform(jax.random.fold_in(own, position), (shards_of,), jnp.float32, smallest / len(shards), top_value / len(shards)))
        loudness = loudness * jnp.repeat(draws, shape[position] // shards_of).reshape([-1 if axis == position else 1 for axis in range(len(shape))])
    return loudness


def normal_values(stream_key, dims, scale, most, shards=(), kind=jnp.bfloat16):
    entries = scale * jax.random.normal(stream_key, dims, jnp.float32)
    if shards:
        entries = entries * block_scale(stream_key, dims, shards, -0.22, 0.18)
    return jnp.clip(entries, -most, most).astype(kind)


def setup_inputs(seed: int = 0, part: int = 0) -> dict:
    arg_keys = jax.random.split(jax.random.key(seed), 10)
    own_keys = jax.random.split(jax.random.fold_in(arg_keys[9], part), 10)
    prefix_kv = draw_prefix_kv(jax.random.fold_in(jax.random.fold_in(arg_keys[9], part), 71), part)
    queries = draw_queries(jax.random.fold_in(jax.random.fold_in(arg_keys[9], part), 71), part)
    new_kv = normal_values(own_keys[2], (2, ROLLOUTS, KVW), 1.0, 6.0, ((1, 16),))
    suffix_kv = normal_values(own_keys[3], (2, ROLLOUTS, SUF, KVW), 1.0, 6.0, ((1, 16),))
    suffix_len = draw_suffix_len(jax.random.fold_in(jax.random.fold_in(arg_keys[9], part), 71), part)
    node_kv = normal_values(own_keys[5], (2, NODES, NODE_LEN, KVW), 1.0, 6.0, ((1, 4),))
    node_len = draw_node_len(jax.random.fold_in(jax.random.fold_in(arg_keys[9], part), 71), part)
    parent = draw_parent(jax.random.fold_in(jax.random.fold_in(arg_keys[9], part), 71), part)
    leaf = touch_ends(jax.random.randint(own_keys[8], (ROLLOUTS,), 0, NODES), jax.random.fold_in(own_keys[8], 1), 0, NODES - 1).astype(jnp.int32)
    return {"prefix_kv": prefix_kv, "queries": queries, "new_kv": new_kv, "suffix_kv": suffix_kv, "suffix_len": suffix_len, "node_kv": node_kv, "node_len": node_len, "parent": parent, "leaf": leaf}


def reference(prefix_kv, queries, new_kv, suffix_kv, suffix_len, node_kv, node_len, parent, leaf):
    group = HEADS // KV_HEADS
    inverse_root = 1.0 / math.sqrt(HEAD_DIM)
    node_ids = jnp.arange(NODES, dtype=jnp.int32)
    current = node_ids
    ancestry = jnp.zeros((NODES, NODES), dtype=bool)
    for climb_step in range(NODES):
        ancestry = ancestry | (current[:, None] == node_ids[None, :])
        current = jnp.where(current >= 0, parent[jnp.maximum(current, 0)], -1).astype(jnp.int32)
    member = ancestry[leaf]
    node_live = jnp.arange(NODE_LEN, dtype=jnp.int32)[None, :] < node_len[:, None]
    prefix_keys = prefix_kv[0].astype(jnp.float32).reshape(PREFIX, KV_HEADS, HEAD_DIM)
    prefix_values = prefix_kv[1].astype(jnp.float32).reshape(PREFIX, KV_HEADS, HEAD_DIM)
    node_keys = node_kv[0].astype(jnp.float32).reshape(NODES * NODE_LEN, KV_HEADS, HEAD_DIM)
    node_values = node_kv[1].astype(jnp.float32).reshape(NODES * NODE_LEN, KV_HEADS, HEAD_DIM)
    suffix_pos = jnp.arange(SUF, dtype=jnp.int32)
    node_tokens = NODES * NODE_LEN

    def one_block(inputs):
        query_rows, member_rows, suffix_keys, suffix_values, lengths, fresh_keys, fresh_values = inputs
        count = query_rows.shape[0]
        query_heads = query_rows.astype(jnp.float32).reshape(count, KV_HEADS, group, HEAD_DIM)
        prefix_scores = jnp.einsum('bhgd,thd->bhgt', query_heads, prefix_keys) * inverse_root
        node_mask = (member_rows[:, :, None] & node_live[None, :, :]).reshape(count, node_tokens)
        node_scores = jnp.einsum('bhgd,thd->bhgt', query_heads, node_keys) * inverse_root
        node_scores = jnp.where(node_mask[:, None, None, :], node_scores, -jnp.inf)
        suffix_keys_f = suffix_keys.astype(jnp.float32)
        suffix_scores = jnp.einsum('bhgd,bshd->bhgs', query_heads, suffix_keys_f) * inverse_root
        suffix_mask = suffix_pos[None, :] < lengths[:, None]
        suffix_scores = jnp.where(suffix_mask[:, None, None, :], suffix_scores, -jnp.inf)
        fresh_scores = jnp.einsum('bhgd,bhd->bhg', query_heads, fresh_keys.astype(jnp.float32))[..., None] * inverse_root
        scores = jnp.concatenate([prefix_scores, node_scores, suffix_scores, fresh_scores], axis=-1)
        peak = lax.optimization_barrier(jnp.max(scores, axis=-1))
        weights = jnp.exp(scores - peak[..., None])
        totals = lax.optimization_barrier(jnp.sum(weights, axis=-1))
        rounded = lax.optimization_barrier(weights.astype(jnp.bfloat16)).astype(jnp.float32)
        mixed = jnp.einsum('bhgt,thd->bhgd', rounded[..., :PREFIX], prefix_values)
        mixed = mixed + jnp.einsum('bhgt,thd->bhgd', rounded[..., PREFIX:PREFIX + node_tokens], node_values)
        mixed = mixed + jnp.einsum('bhgs,bshd->bhgd', rounded[..., PREFIX + node_tokens:PREFIX + node_tokens + SUF], suffix_values.astype(jnp.float32))
        mixed = mixed + rounded[..., -1:] * fresh_values.astype(jnp.float32)[:, :, None, :]
        return (mixed / totals[..., None]).astype(jnp.bfloat16).reshape(count, QW)
    blocks = ROLLOUTS // R_DEV
    inputs = (queries.reshape(blocks, R_DEV, QW), member.reshape(blocks, R_DEV, NODES), suffix_kv[0].reshape(blocks, R_DEV, SUF, KV_HEADS, HEAD_DIM), suffix_kv[1].reshape(blocks, R_DEV, SUF, KV_HEADS, HEAD_DIM), suffix_len.reshape(blocks, R_DEV), new_kv[0].reshape(blocks, R_DEV, KV_HEADS, HEAD_DIM), new_kv[1].reshape(blocks, R_DEV, KV_HEADS, HEAD_DIM))
    return lax.map(one_block, inputs).reshape(ROLLOUTS, QW)
```

```python
import functools
import math

import jax
import jax.numpy as jnp
from jax import lax
from jax.experimental import pallas as pl
from jax.experimental.pallas import tpu as pltpu
from jax.sharding import PartitionSpec as P

HEADS = 64
KV_HEADS = 8
HEAD_DIM = 128
NODE_LEN = 128
GROUP = HEADS // KV_HEADS
GW = GROUP * HEAD_DIM
MESH = pl.DeviceIdType.MESH
LOG2E = math.log2(math.e)
COEF = HEAD_DIM ** (-0.5) * LOG2E


def dot_t(keys, rows):
    return lax.dot_general(keys, rows, (((1,), (1,)), ((), ())), preferred_element_type=jnp.float32)


def kernel(
    n, nb, suffix_len, node_len, parent, leaf, q_ref, new_ref, prefix_hbm, suffix_hbm, node_hbm, out_ref,
    prefix, suffix, nodes, vt, qg, o_out, l_out, o_in, l_in, o_loc, l_loc,
    load_sem, q_send, q_recv, r_send, r_recv, l_send, l_recv, n_send, n_recv,
):
    c = lax.axis_index("ctx")
    b = lax.axis_index("branch")
    rollouts = q_ref.shape[0]
    rows = rollouts * GROUP
    node_count = node_len.shape[0]
    suf = suffix.shape[2]

    load_k = pltpu.make_async_copy(prefix_hbm, prefix, load_sem.at[0])
    load_s = pltpu.make_async_copy(suffix_hbm, suffix, load_sem.at[1])
    load_n = pltpu.make_async_copy(node_hbm, nodes.at[b], load_sem.at[2])
    load_k.start()
    load_s.start()
    load_n.start()

    barrier = pltpu.get_barrier_semaphore()
    for k in range(1, n):
        pl.semaphore_signal(barrier, inc=1, device_id={"ctx": lax.rem(c + k, n)}, device_id_type=MESH)
    for k in range(1, nb):
        pl.semaphore_signal(barrier, inc=1, device_id={"branch": lax.rem(b + k, nb)}, device_id_type=MESH)
    pl.semaphore_wait(barrier, n - 1 + nb - 1)

    def cols(g):
        return pl.ds(pl.multiple_of(g * GW, GW), GW)

    def head_cols(g):
        return pl.ds(pl.multiple_of(g * HEAD_DIM, HEAD_DIM), HEAD_DIM)

    def own_copy(side, target, g):
        return pltpu.make_async_remote_copy(
            src_ref=q_ref.at[:, cols(g)], dst_ref=qg.at[c, :, cols(g)],
            send_sem=q_send.at[side, c, g], recv_sem=q_recv.at[c, g],
            device_id={"ctx": target}, device_id_type=MESH)

    def pass_copy(side, src, target, g):
        return pltpu.make_async_remote_copy(
            src_ref=qg.at[src, :, cols(g)], dst_ref=qg.at[src, :, cols(g)],
            send_sem=q_send.at[side, src, g], recv_sem=q_recv.at[src, g],
            device_id={"ctx": target}, device_id_type=MESH)

    def result_copy(peer, slot, g):
        return pltpu.make_async_remote_copy(
            src_ref=o_out.at[peer, g], dst_ref=o_in.at[slot, g],
            send_sem=r_send.at[peer, g], recv_sem=r_recv.at[slot, g],
            device_id={"ctx": peer}, device_id_type=MESH)

    def stat_copy(peer, slot):
        return pltpu.make_async_remote_copy(
            src_ref=l_out.at[peer], dst_ref=l_in.at[slot],
            send_sem=l_send.at[peer], recv_sem=l_recv.at[slot],
            device_id={"ctx": peer}, device_id_type=MESH)

    def node_copy(peer, slot, k):
        return pltpu.make_async_remote_copy(
            src_ref=node_hbm, dst_ref=nodes.at[slot],
            send_sem=n_send.at[k], recv_sem=n_recv.at[slot],
            device_id={"branch": peer}, device_id_type=MESH)

    @pl.loop(0, KV_HEADS)
    def _(g):
        @pl.when(c + 1 < n)
        def _():
            own_copy(0, c + 1, g).start()

        @pl.when(c >= 1)
        def _():
            own_copy(1, c - 1, g).start()

    for k in range(1, nb):
        node_copy(lax.rem(b + k, nb), b, k).start()

    lane = lax.rem(lax.broadcasted_iota(jnp.int32, (1, rows), 1), rollouts)
    lengths = jnp.zeros((1, rows), jnp.int32)
    current = jnp.zeros((1, rows), jnp.int32)
    for r in range(rollouts):
        lengths = jnp.where(lane == r, suffix_len[r], lengths)
        current = jnp.where(lane == r, leaf[r], current)
    limits = [jnp.zeros((1, rows), jnp.int32) for _ in range(node_count)]
    for _ in range(node_count):
        lifted = jnp.full((1, rows), -1, jnp.int32)
        for node in range(node_count):
            hit = current == node
            limits[node] = jnp.where(hit, node_len[node], limits[node])
            lifted = jnp.where(hit, parent[node], lifted)
        current = lifted
    first = lane * suf
    last = first + lengths

    def stack(block):
        return jnp.concatenate(
            [block[:, j * HEAD_DIM:(j + 1) * HEAD_DIM] for j in range(GROUP)], axis=0)

    def prefix_item(query, g, values_t):
        keys = prefix[0, :, head_cols(g)]
        scores = dot_t(keys, query)
        peak = jnp.max(scores, axis=0, keepdims=True) * COEF
        weights = jnp.exp2(scores * COEF - peak)
        total = jnp.sum(weights, axis=0, keepdims=True)
        mixed = jnp.dot(values_t, weights.astype(jnp.bfloat16), preferred_element_type=jnp.float32)
        return mixed / total, peak + jnp.log2(total)

    def serve(src, g, onward, ok):
        pass_copy(0, src, src, g).wait_recv()

        @pl.when(ok)
        def _():
            pass_copy(onward[0], src, onward[1], g).start()

        mixed, stat = prefix_item(stack(qg[src, :, cols(g)]), g, vt[g])
        o_out[src, g] = mixed.astype(jnp.bfloat16)
        l_out[src, pl.ds(g, 1), :] = stat
        result_copy(src, c, g).start()

        @pl.when(g == KV_HEADS - 1)
        def _():
            stat_copy(src, c).start()

    def local_item(g):
        query = stack(q_ref[:, cols(g)])
        pieces = []
        keys = suffix[0, :, :, head_cols(g)].reshape(rollouts * suf, HEAD_DIM)
        token = lax.broadcasted_iota(jnp.int32, (rollouts * suf, rows), 0)
        scores = jnp.where((token >= first) & (token < last), dot_t(keys, query), -jnp.inf)
        pieces.append((scores, suffix[1, :, :, head_cols(g)].reshape(rollouts * suf, HEAD_DIM)))
        spot = lax.broadcasted_iota(jnp.int32, (NODE_LEN, rows), 0)
        for node in range(node_count):
            owner, inner = node // nodes.shape[2], node % nodes.shape[2]
            scores = dot_t(nodes[owner, 0, inner, :, head_cols(g)], query)
            scores = jnp.where(spot < limits[node], scores, -jnp.inf)
            pieces.append((scores, nodes[owner, 1, inner, :, head_cols(g)]))
        spot = lax.broadcasted_iota(jnp.int32, (rollouts, rows), 0)
        scores = jnp.where(spot == lane, dot_t(new_ref[0, :, head_cols(g)], query), -jnp.inf)
        pieces.append((scores, new_ref[1, :, head_cols(g)]))
        peak = functools.reduce(jnp.maximum, [jnp.max(s, axis=0, keepdims=True) for s, _ in pieces]) * COEF
        total, mixed = 0.0, 0.0
        for scores, values in pieces:
            weights = jnp.exp2(scores * COEF - peak)
            total = total + jnp.sum(weights, axis=0, keepdims=True)
            mixed = mixed + lax.dot_general(
                values, weights.astype(jnp.bfloat16), (((0,), (0,)), ((), ())),
                preferred_element_type=jnp.float32)
        return mixed / total, peak + jnp.log2(total)

    load_k.wait()

    @pl.loop(0, KV_HEADS * max(n - 1, 2))
    def _(t):
        d = t // KV_HEADS + 1
        g = lax.rem(t, KV_HEADS)

        @pl.when(d == 1)
        def _():
            values_t = prefix[1, :, head_cols(g)].T
            vt[g] = values_t
            mixed, stat = prefix_item(stack(q_ref[:, cols(g)]), g, values_t)
            o_loc[0, g] = mixed
            l_loc[0, pl.ds(g, 1), :] = stat

        @pl.when(c - d >= 0)
        def _():
            serve(c - d, g, (0, c + 1), c + 1 < n)

        @pl.when(c + d < n)
        def _():
            serve(c + d, g, (1, c - 1), c >= 1)

        @pl.when(t == KV_HEADS)
        def _():
            load_s.wait()
            load_n.wait()
            for k in range(1, nb):
                node_copy(b, lax.rem(b + k, nb), k).wait_recv()

        @pl.when(d == 2)
        def _():
            mixed, stat = local_item(g)
            o_loc[1, g] = mixed
            l_loc[1, pl.ds(g, 1), :] = stat

    for k in range(1, n):
        stat_copy(c, lax.rem(c + k, n)).wait_recv()

    @pl.loop(0, KV_HEADS)
    def _(g):
        stats = [l_loc[0, pl.ds(g, 1), :], l_loc[1, pl.ds(g, 1), :]]
        for k in range(1, n):
            stats.append(l_in[lax.rem(c + k, n), pl.ds(g, 1), :])
        peak = functools.reduce(jnp.maximum, stats)
        shares = [jnp.exp2(stat - peak) for stat in stats]
        scale = 1.0 / functools.reduce(jnp.add, shares)
        mixed = o_loc[0, g] * (shares[0] * scale) + o_loc[1, g] * (shares[1] * scale)
        for k in range(1, n):
            slot = lax.rem(c + k, n)
            result_copy(c, slot, g).wait_recv()
            mixed = mixed + o_in[slot, g].astype(jnp.float32) * (shares[k + 1] * scale)
        done = mixed.T.astype(jnp.bfloat16)
        for j in range(GROUP):
            out_ref[:, pl.ds(pl.multiple_of(g * GW + j * HEAD_DIM, HEAD_DIM), HEAD_DIM)] = (
                done[j * rollouts:(j + 1) * rollouts])

    @pl.loop(0, KV_HEADS)
    def _(g):
        @pl.when(c + 1 < n)
        def _():
            own_copy(0, c + 1, g).wait_send()

        @pl.when(c >= 1)
        def _():
            own_copy(1, c - 1, g).wait_send()

        for d in range(1, n):
            @pl.when((c - d >= 0) & (c + 1 < n))
            def _():
                pass_copy(0, c - d, c + 1, g).wait_send()

            @pl.when((c + d < n) & (c >= 1))
            def _():
                pass_copy(1, c + d, c - 1, g).wait_send()

            result_copy(lax.rem(c + d, n), c, g).wait_send()

    for k in range(1, n):
        stat_copy(lax.rem(c + k, n), c).wait_send()
    for k in range(1, nb):
        node_copy(lax.rem(b + k, nb), b, k).wait_send()


def on_device(n, nb, prefix_kv, queries, new_kv, suffix_kv, suffix_len, node_kv, node_len, parent, leaf):
    rows = queries.shape[0] * GROUP
    smem = pl.BlockSpec(memory_space=pltpu.SMEM)
    vmem = pl.BlockSpec(memory_space=pltpu.VMEM)
    hbm = pl.BlockSpec(memory_space=pl.ANY)
    dma = pltpu.SemaphoreType.DMA
    bf16, f32 = jnp.bfloat16, jnp.float32
    return pl.pallas_call(
        functools.partial(kernel, n, nb),
        out_shape=jax.ShapeDtypeStruct(queries.shape, bf16),
        in_specs=[smem] * 4 + [vmem] * 2 + [hbm] * 3,
        out_specs=vmem,
        scratch_shapes=[
            pltpu.VMEM(prefix_kv.shape, bf16),
            pltpu.VMEM(suffix_kv.shape, bf16),
            pltpu.VMEM((nb,) + node_kv.shape, bf16),
            pltpu.VMEM((KV_HEADS, HEAD_DIM, prefix_kv.shape[1]), bf16),
            pltpu.VMEM((n,) + queries.shape, bf16),
            pltpu.VMEM((n, KV_HEADS, HEAD_DIM, rows), bf16),
            pltpu.VMEM((n, KV_HEADS, rows), f32),
            pltpu.VMEM((n, KV_HEADS, HEAD_DIM, rows), bf16),
            pltpu.VMEM((n, KV_HEADS, rows), f32),
            pltpu.VMEM((2, KV_HEADS, HEAD_DIM, rows), f32),
            pltpu.VMEM((2, KV_HEADS, rows), f32),
            dma((3,)),
            dma((2, n, KV_HEADS)),
            dma((n, KV_HEADS)),
            dma((n, KV_HEADS)),
            dma((n, KV_HEADS)),
            dma((n,)),
            dma((n,)),
            dma((nb,)),
            dma((nb,)),
        ],
        compiler_params=pltpu.CompilerParams(
            collective_id=0, has_side_effects=True, vmem_limit_bytes=50 * 1024 * 1024),
    )(suffix_len, node_len, parent, leaf, queries, new_kv, prefix_kv, suffix_kv, node_kv)


def solution(mesh):
    return jax.shard_map(
        functools.partial(on_device, mesh.shape["ctx"], mesh.shape["branch"]),
        mesh=mesh,
        in_specs=(
            P(None, ("parts", "ctx"), None),
            P(("parts", "ctx", "branch"), None),
            P(None, ("parts", "ctx", "branch"), None),
            P(None, ("parts", "ctx", "branch"), None, None),
            P(("parts", "ctx", "branch")),
            P(None, ("parts", "branch"), None, None),
            P("parts"),
            P("parts"),
            P(("parts", "ctx", "branch")),
        ),
        out_specs=P(("parts", "ctx", "branch"), None),
        check_vma=False,
    )
```

```python
import functools
import math

import jax
import jax.numpy as jnp
from jax import lax
from jax.experimental import pallas as pl
from jax.experimental.pallas import tpu as pltpu
from jax.sharding import PartitionSpec as P

HEADS = 64
KV_HEADS = 8
HEAD_DIM = 128
NODE_LEN = 128
GROUP = HEADS // KV_HEADS
GW = GROUP * HEAD_DIM
MESH = pl.DeviceIdType.MESH
LOG2E = math.log2(math.e)
COEF = HEAD_DIM ** (-0.5) * LOG2E


def dot_t(keys, rows):
    return lax.dot_general(keys, rows, (((1,), (1,)), ((), ())), preferred_element_type=jnp.float32)
LAG = 2


def kernel(
    n, nb, suffix_len_hbm, node_len_hbm, parent_hbm, leaf_hbm, q_hbm, new_hbm, prefix_hbm, suffix_hbm, node_hbm,
    out_ref,
    suffix_len, node_len, parent, leaf, new_ref, prefix, suffix, nodes, vt, qg,
    o_part, l_part, o_out, l_out, o_in, l_in, o_loc, l_loc,
    load_sem, q_send, q_recv, r_send, r_recv, l_send, l_recv, n_send, n_pass, n_recv,
):
    c = lax.axis_index("ctx")
    b = lax.axis_index("branch")
    rollouts = qg.shape[1]
    rows = rollouts * GROUP
    node_count = node_len.shape[0]
    suf = suffix.shape[2]
    chips = nb // 2
    core = lax.rem(b, 2)
    twin = b + 1 - 2 * core

    loads = [
        pltpu.make_async_copy(src, dst, load_sem.at[i])
        for i, (src, dst) in enumerate([
            (q_hbm, qg.at[c]), (prefix_hbm, prefix), (suffix_hbm, suffix), (node_hbm, nodes.at[b]),
            (new_hbm, new_ref), (suffix_len_hbm, suffix_len), (node_len_hbm, node_len),
            (parent_hbm, parent), (leaf_hbm, leaf)])
    ]
    for load in loads:
        load.start()

    barrier = pltpu.get_barrier_semaphore()
    for k in range(1, n):
        pl.semaphore_signal(barrier, inc=1, device_id={"ctx": lax.rem(c + k, n)}, device_id_type=MESH)
    for k in range(1, nb):
        pl.semaphore_signal(barrier, inc=1, device_id={"branch": lax.rem(b + k, nb)}, device_id_type=MESH)
    pl.semaphore_wait(barrier, n - 1 + nb - 1)

    def cols(g):
        return pl.ds(pl.multiple_of(g * GW, GW), GW)

    def head_cols(g):
        return pl.ds(pl.multiple_of(g * HEAD_DIM, HEAD_DIM), HEAD_DIM)

    def own_copy(side, target, g):
        return pltpu.make_async_remote_copy(
            src_ref=q_hbm.at[:, cols(g)], dst_ref=qg.at[c, :, cols(g)],
            send_sem=q_send.at[side, c, g], recv_sem=q_recv.at[c, g],
            device_id={"ctx": target}, device_id_type=MESH)

    def pass_copy(side, src, target, g):
        return pltpu.make_async_remote_copy(
            src_ref=qg.at[src, :, cols(g)], dst_ref=qg.at[src, :, cols(g)],
            send_sem=q_send.at[side, src, g], recv_sem=q_recv.at[src, g],
            device_id={"ctx": target}, device_id_type=MESH)

    def result_copies(dest, side, target, g):
        return (
            pltpu.make_async_remote_copy(
                src_ref=o_out.at[dest, g], dst_ref=o_in.at[side, dest, g],
                send_sem=r_send.at[dest, g], recv_sem=r_recv.at[side, dest, g],
                device_id={"ctx": target}, device_id_type=MESH),
            pltpu.make_async_remote_copy(
                src_ref=l_out.at[dest, g], dst_ref=l_in.at[side, dest, g],
                send_sem=l_send.at[dest, g], recv_sem=l_recv.at[side, dest, g],
                device_id={"ctx": target}, device_id_type=MESH))

    def node_copy(peer, slot, sem):
        return pltpu.make_async_remote_copy(
            src_ref=node_hbm, dst_ref=nodes.at[slot], send_sem=sem, recv_sem=n_recv.at[slot],
            device_id={"branch": peer}, device_id_type=MESH)

    def node_pass(slot, sem):
        return pltpu.make_async_remote_copy(
            src_ref=nodes.at[slot], dst_ref=nodes.at[slot], send_sem=sem, recv_sem=n_recv.at[slot],
            device_id={"branch": twin}, device_id_type=MESH)

    @pl.loop(0, KV_HEADS)
    def _(g):
        @pl.when(c + 1 < n)
        def _():
            own_copy(0, c + 1, g).start()

        @pl.when(c >= 1)
        def _():
            own_copy(1, c - 1, g).start()

    for k in range(1, chips):
        node_copy(lax.rem(b + 2 * k, nb), b, n_send.at[k]).start()
    node_copy(twin, b, n_send.at[0]).start()

    for load in loads[5:]:
        load.wait()
    lane = lax.rem(lax.broadcasted_iota(jnp.int32, (1, rows), 1), rollouts)
    lengths = jnp.zeros((1, rows), jnp.int32)
    current = jnp.zeros((1, rows), jnp.int32)
    for r in range(rollouts):
        lengths = jnp.where(lane == r, suffix_len[r], lengths)
        current = jnp.where(lane == r, leaf[r], current)
    limits = [jnp.zeros((1, rows), jnp.int32) for _ in range(node_count)]
    for _ in range(node_count):
        lifted = jnp.full((1, rows), -1, jnp.int32)
        for node in range(node_count):
            hit = current == node
            limits[node] = jnp.where(hit, node_len[node], limits[node])
            lifted = jnp.where(hit, parent[node], lifted)
        current = lifted
    first = lane * suf
    last = first + lengths

    def stack(block):
        return [block[:, j * HEAD_DIM:(j + 1) * HEAD_DIM] for j in range(GROUP)]

    def ranked(k):
        near = jnp.minimum(c, n - 1 - c)
        by_two = c - (k + 1) // 2 if k % 2 else c + (k + 1) // 2
        single = jnp.where(2 * c > n - 1, c - (k - near), c + (k - near))
        return jnp.where(k <= 2 * near, by_two, single)

    def pump(d, g):
        @pl.when(c - d >= 0)
        def _():
            pass_copy(0, c - d, c - d, g).wait_recv()

            @pl.when(c + 1 < n)
            def _():
                pass_copy(0, c - d, c + 1, g).start()

        @pl.when(c + d < n)
        def _():
            pass_copy(1, c + d, c + d, g).wait_recv()

            @pl.when(c >= 1)
            def _():
                pass_copy(1, c + d, c - 1, g).start()

    def send(dest, g, mixed, stat):
        o_out[dest, g] = mixed.astype(jnp.bfloat16)
        l_out[dest, g] = stat

        @pl.when(dest < c)
        def _():
            for copy in result_copies(dest, 0, c - 1, g):
                copy.start()

        @pl.when(dest > c)
        def _():
            for copy in result_copies(dest, 1, c + 1, g):
                copy.start()

    def emit(dest, g, mixed, stat):
        edge = ((dest < c) & (c == n - 1)) | ((dest > c) & (c == 0))

        @pl.when(edge)
        def _():
            send(dest, g, mixed, stat)

        @pl.when(jnp.logical_not(edge))
        def _():
            o_part[dest, g] = mixed
            l_part[dest, g] = stat

    def pair_item(pair, g):
        for d in (2 * pair, 2 * pair + 1):
            if d:
                pump(d, g)
        one, two = (ranked(2 * pair) if pair else c), ranked(2 * pair + 1)
        query = jnp.concatenate(stack(qg[one, :, cols(g)]) + stack(qg[two, :, cols(g)]), axis=0)
        if pair == 0:
            vt[g] = prefix[1, :, head_cols(g)].T
        scores = dot_t(prefix[0, :, head_cols(g)], query)
        peak = jnp.max(scores, axis=0, keepdims=True) * COEF
        weights = jnp.exp2(scores * COEF - peak)
        total = jnp.sum(weights, axis=0, keepdims=True)
        mixed = jnp.dot(vt[g], weights.astype(jnp.bfloat16), preferred_element_type=jnp.float32)
        mixed = mixed * (1.0 / total)
        stat = peak + jnp.log2(total)
        if pair:
            emit(one, g, mixed[:, :rows], stat[:, :rows])
        else:
            o_loc[0, g] = mixed[:, :rows]
            l_loc[0, g] = stat[:, :rows]
        emit(two, g, mixed[:, rows:], stat[:, rows:])

    def merge(dest, side, g):
        for copy in result_copies(dest, side, dest, g):
            copy.wait_recv()
        stat_a, stat_b = l_part[dest, g], l_in[side, dest, g]
        peak = jnp.maximum(stat_a, stat_b)
        share_a, share_b = jnp.exp2(stat_a - peak), jnp.exp2(stat_b - peak)
        total = share_a + share_b
        scale = 1.0 / total
        mixed = o_part[dest, g] * (share_a * scale) + o_in[side, dest, g].astype(jnp.float32) * (share_b * scale)
        send(dest, g, mixed, peak + jnp.log2(total))

    def local_item(g):
        query = jnp.concatenate(stack(qg[c, :, cols(g)]), axis=0)
        pieces = []
        keys = suffix[0, :, :, head_cols(g)].reshape(rollouts * suf, HEAD_DIM)
        token = lax.broadcasted_iota(jnp.int32, (rollouts * suf, rows), 0)
        scores = jnp.where((token >= first) & (token < last), dot_t(keys, query), -jnp.inf)
        pieces.append((scores, suffix[1, :, :, head_cols(g)].reshape(rollouts * suf, HEAD_DIM)))
        spot = lax.broadcasted_iota(jnp.int32, (NODE_LEN, rows), 0)
        for node in range(node_count):
            owner, inner = node // nodes.shape[2], node % nodes.shape[2]
            scores = dot_t(nodes[owner, 0, inner, :, head_cols(g)], query)
            scores = jnp.where(spot < limits[node], scores, -jnp.inf)
            pieces.append((scores, nodes[owner, 1, inner, :, head_cols(g)]))
        spot = lax.broadcasted_iota(jnp.int32, (rollouts, rows), 0)
        scores = jnp.where(spot == lane, dot_t(new_ref[0, :, head_cols(g)], query), -jnp.inf)
        pieces.append((scores, new_ref[1, :, head_cols(g)]))
        peak = functools.reduce(jnp.maximum, [jnp.max(s, axis=0, keepdims=True) for s, _ in pieces]) * COEF
        total, mixed = 0.0, 0.0
        for scores, values in pieces:
            weights = jnp.exp2(scores * COEF - peak)
            total = total + jnp.sum(weights, axis=0, keepdims=True)
            mixed = mixed + lax.dot_general(
                values, weights.astype(jnp.bfloat16), (((0,), (0,)), ((), ())),
                preferred_element_type=jnp.float32)
        return mixed / total, peak + jnp.log2(total)

    loads[0].wait()
    loads[1].wait()
    for pair in range(n // 2 - 1):
        @pl.loop(0, KV_HEADS)
        def _(g):
            pair_item(pair, g)

    @pl.loop(0, max(2 * KV_HEADS, KV_HEADS + LAG * (n - 2)))
    def _(t):
        @pl.when(t < KV_HEADS)
        def _():
            pair_item(n // 2 - 1, t)

        for ring in range(1, n - 1):
            g = t - LAG * ring

            @pl.when((g >= 0) & (g < KV_HEADS))
            def _():
                @pl.when(c == n - 1 - ring)
                def _():
                    for dest in range(n - 1 - ring):
                        merge(dest, 0, g)

                @pl.when(c == ring)
                def _():
                    for dest in range(ring + 1, n):
                        merge(dest, 1, g)

        @pl.when(t == KV_HEADS - 2)
        def _():
            for k in range(1, chips):
                slot = lax.rem(b + 2 * k, nb)
                node_pass(slot, n_pass.at[k]).wait_recv()
                node_pass(slot, n_pass.at[k]).start()

        @pl.when(t == KV_HEADS)
        def _():
            for load in loads[2:5]:
                load.wait()
            for k in range(chips):
                slot = lax.rem(twin + 2 * k, nb)
                node_pass(slot, n_pass.at[k]).wait_recv()

        @pl.when((t >= KV_HEADS) & (t < 2 * KV_HEADS))
        def _():
            g = t - KV_HEADS
            mixed, stat = local_item(g)
            o_loc[1, g] = mixed
            l_loc[1, g] = stat

    @pl.loop(0, KV_HEADS)
    def _(g):
        for side, alone in ((0, c == n - 1), (1, c == 0)):
            @pl.when(alone)
            def _():
                o_in[side, c, g] = jnp.zeros((HEAD_DIM, rows), jnp.bfloat16)
                l_in[side, c, g] = jnp.full((1, rows), -jnp.inf, jnp.float32)

            @pl.when(jnp.logical_not(alone))
            def _():
                for copy in result_copies(c, side, c, g):
                    copy.wait_recv()

        stats = [l_loc[0, g], l_loc[1, g], l_in[0, c, g], l_in[1, c, g]]
        parts = [o_loc[0, g], o_loc[1, g], o_in[0, c, g], o_in[1, c, g]]
        peak = functools.reduce(jnp.maximum, stats)
        shares = [jnp.exp2(stat - peak) for stat in stats]
        scale = 1.0 / functools.reduce(jnp.add, shares)
        mixed = functools.reduce(
            jnp.add, [part.astype(jnp.float32) * (share * scale) for part, share in zip(parts, shares)])
        done = mixed.T.astype(jnp.bfloat16)
        for j in range(GROUP):
            out_ref[:, pl.ds(pl.multiple_of(g * GW + j * HEAD_DIM, HEAD_DIM), HEAD_DIM)] = (
                done[j * rollouts:(j + 1) * rollouts])

    @pl.loop(0, KV_HEADS)
    def _(g):
        @pl.when(c + 1 < n)
        def _():
            own_copy(0, c + 1, g).wait_send()

        @pl.when(c >= 1)
        def _():
            own_copy(1, c - 1, g).wait_send()

        for d in range(1, n):
            @pl.when((c - d >= 0) & (c + 1 < n))
            def _():
                pass_copy(0, c - d, c + 1, g).wait_send()

            @pl.when((c + d < n) & (c >= 1))
            def _():
                pass_copy(1, c + d, c - 1, g).wait_send()

            for copy in result_copies(lax.rem(c + d, n), 0, lax.rem(c + d, n), g):
                copy.wait_send()

    for k in range(1, chips):
        node_copy(lax.rem(b + 2 * k, nb), b, n_send.at[k]).wait_send()
        node_pass(lax.rem(b + 2 * k, nb), n_pass.at[k]).wait_send()
    node_copy(twin, b, n_send.at[0]).wait_send()


def on_device(n, nb, prefix_kv, queries, new_kv, suffix_kv, suffix_len, node_kv, node_len, parent, leaf):
    rows = queries.shape[0] * GROUP
    dma = pltpu.SemaphoreType.DMA
    bf16, f32 = jnp.bfloat16, jnp.float32
    return pl.pallas_call(
        functools.partial(kernel, n, nb),
        out_shape=jax.ShapeDtypeStruct(queries.shape, bf16),
        in_specs=[pl.BlockSpec(memory_space=pltpu.HBM)] * 9,
        out_specs=pl.BlockSpec(memory_space=pltpu.VMEM),
        scratch_shapes=[
            pltpu.SMEM(suffix_len.shape, jnp.int32),
            pltpu.SMEM(node_len.shape, jnp.int32),
            pltpu.SMEM(parent.shape, jnp.int32),
            pltpu.SMEM(leaf.shape, jnp.int32),
            pltpu.VMEM(new_kv.shape, bf16),
            pltpu.VMEM(prefix_kv.shape, bf16),
            pltpu.VMEM(suffix_kv.shape, bf16),
            pltpu.VMEM((nb,) + node_kv.shape, bf16),
            pltpu.VMEM((KV_HEADS, HEAD_DIM, prefix_kv.shape[1]), bf16),
            pltpu.VMEM((n,) + queries.shape, bf16),
            pltpu.VMEM((n, KV_HEADS, HEAD_DIM, rows), f32),
            pltpu.VMEM((n, KV_HEADS, 1, rows), f32),
            pltpu.VMEM((n, KV_HEADS, HEAD_DIM, rows), bf16),
            pltpu.VMEM((n, KV_HEADS, 1, rows), f32),
            pltpu.VMEM((2, n, KV_HEADS, HEAD_DIM, rows), bf16),
            pltpu.VMEM((2, n, KV_HEADS, 1, rows), f32),
            pltpu.VMEM((2, KV_HEADS, HEAD_DIM, rows), f32),
            pltpu.VMEM((2, KV_HEADS, 1, rows), f32),
            dma((9,)),
            dma((2, n, KV_HEADS)),
            dma((n, KV_HEADS)),
            dma((n, KV_HEADS)),
            dma((2, n, KV_HEADS)),
            dma((n, KV_HEADS)),
            dma((2, n, KV_HEADS)),
            dma((nb // 2,)),
            dma((nb // 2,)),
            dma((nb,)),
        ],
        compiler_params=pltpu.CompilerParams(
            collective_id=0, has_side_effects=True, vmem_limit_bytes=63 * 1024 * 1024),
    )(suffix_len, node_len, parent, leaf, queries, new_kv, prefix_kv, suffix_kv, node_kv)


def solution(mesh):
    return jax.shard_map(
        functools.partial(on_device, mesh.shape["ctx"], mesh.shape["branch"]),
        mesh=mesh,
        in_specs=(
            P(None, ("parts", "ctx"), None),
            P(("parts", "ctx", "branch"), None),
            P(None, ("parts", "ctx", "branch"), None),
            P(None, ("parts", "ctx", "branch"), None, None),
            P(("parts", "ctx", "branch")),
            P(None, ("parts", "branch"), None, None),
            P("parts"),
            P("parts"),
            P(("parts", "ctx", "branch")),
        ),
        out_specs=P(("parts", "ctx", "branch"), None),
        check_vma=False,
    )
```

```python
import functools
import math

import jax
import jax.numpy as jnp
from jax import lax
from jax.experimental import pallas as pl
from jax.experimental.pallas import tpu as pltpu
from jax.sharding import PartitionSpec as P

HEADS = 64
KV_HEADS = 8
HEAD_DIM = 128
NODE_LEN = 128
GROUP = HEADS // KV_HEADS
GW = GROUP * HEAD_DIM
MESH = pl.DeviceIdType.MESH
LOG2E = math.log2(math.e)
COEF = HEAD_DIM ** (-0.5) * LOG2E


def dot_t(keys, rows):
    return lax.dot_general(keys, rows, (((1,), (1,)), ((), ())), preferred_element_type=jnp.float32)
LAG = 4
STEP = 4


def kernel(
    n, nb, suffix_len_hbm, node_len_hbm, parent_hbm, leaf_hbm, q_hbm, new_hbm, prefix_hbm, suffix_hbm, node_hbm,
    out_ref,
    suffix_len, node_len, parent, leaf, new_ref, prefix, suffix, nodes, vt, qg,
    o_part, l_part, o_out, l_out, o_in, l_in, o_loc, l_loc,
    load_sem, q_send, q_recv, r_send, r_recv, l_send, l_recv, n_send, n_pass, n_recv,
):
    c = lax.axis_index("ctx")
    b = lax.axis_index("branch")
    rollouts = qg.shape[1]
    rows = rollouts * GROUP
    node_count = node_len.shape[0]
    suf = suffix.shape[2]
    chips = nb // 2
    core = lax.rem(b, 2)
    twin = b + 1 - 2 * core

    loads = [
        pltpu.make_async_copy(src, dst, load_sem.at[i])
        for i, (src, dst) in enumerate([
            (q_hbm, qg.at[c]), (prefix_hbm, prefix), (suffix_hbm, suffix), (node_hbm, nodes.at[b]),
            (new_hbm, new_ref), (suffix_len_hbm, suffix_len), (node_len_hbm, node_len),
            (parent_hbm, parent), (leaf_hbm, leaf)])
    ]
    for load in loads:
        load.start()

    barrier = pltpu.get_barrier_semaphore()
    @pl.when(c + 1 < n)
    def _():
        pl.semaphore_signal(barrier, inc=1, device_id={"ctx": c + 1}, device_id_type=MESH)

    @pl.when(c >= 1)
    def _():
        pl.semaphore_signal(barrier, inc=1, device_id={"ctx": c - 1}, device_id_type=MESH)

    pl.semaphore_signal(barrier, inc=1, device_id={"branch": twin}, device_id_type=MESH)
    for k in range(1, chips):
        pl.semaphore_signal(barrier, inc=1, device_id={"branch": lax.rem(b + 2 * k, nb)}, device_id_type=MESH)

    @pl.when((c >= 1) & (c + 1 < n))
    def _():
        pl.semaphore_wait(barrier, chips + 2)

    @pl.when((c == 0) | (c == n - 1))
    def _():
        pl.semaphore_wait(barrier, chips + 1)

    def cols(g):
        return pl.ds(pl.multiple_of(g * GW, GW), GW)

    def head_cols(g):
        return pl.ds(pl.multiple_of(g * HEAD_DIM, HEAD_DIM), HEAD_DIM)

    def own_copy(side, target, g):
        return pltpu.make_async_remote_copy(
            src_ref=q_hbm.at[:, cols(g)], dst_ref=qg.at[c, :, cols(g)],
            send_sem=q_send.at[side, c, g], recv_sem=q_recv.at[c, g],
            device_id={"ctx": target}, device_id_type=MESH)

    def pass_copy(side, src, target, g):
        return pltpu.make_async_remote_copy(
            src_ref=qg.at[src, :, cols(g)], dst_ref=qg.at[src, :, cols(g)],
            send_sem=q_send.at[side, src, g], recv_sem=q_recv.at[src, g],
            device_id={"ctx": target}, device_id_type=MESH)

    def result_copies(dest, side, target, g):
        return (
            pltpu.make_async_remote_copy(
                src_ref=o_out.at[dest, g], dst_ref=o_in.at[side, dest, g],
                send_sem=r_send.at[dest, g], recv_sem=r_recv.at[side, dest, g],
                device_id={"ctx": target}, device_id_type=MESH),
            pltpu.make_async_remote_copy(
                src_ref=l_out.at[dest, g], dst_ref=l_in.at[side, dest, g],
                send_sem=l_send.at[dest, g], recv_sem=l_recv.at[side, dest, g],
                device_id={"ctx": target}, device_id_type=MESH))

    def node_copy(peer, slot, sem):
        return pltpu.make_async_remote_copy(
            src_ref=node_hbm, dst_ref=nodes.at[slot], send_sem=sem, recv_sem=n_recv.at[slot],
            device_id={"branch": peer}, device_id_type=MESH)

    def node_pass(slot, sem):
        return pltpu.make_async_remote_copy(
            src_ref=nodes.at[slot], dst_ref=nodes.at[slot], send_sem=sem, recv_sem=n_recv.at[slot],
            device_id={"branch": twin}, device_id_type=MESH)

    @pl.loop(0, KV_HEADS)
    def _(g):
        @pl.when(c + 1 < n)
        def _():
            own_copy(0, c + 1, g).start()

        @pl.when(c >= 1)
        def _():
            own_copy(1, c - 1, g).start()

    for k in range(1, chips):
        node_copy(lax.rem(b + 2 * k, nb), b, n_send.at[k]).start()
    node_copy(twin, b, n_send.at[0]).start()

    for load in loads[5:]:
        load.wait()
    lane = lax.rem(lax.broadcasted_iota(jnp.int32, (1, rows), 1), rollouts)
    lengths = jnp.zeros((1, rows), jnp.int32)
    current = jnp.zeros((1, rows), jnp.int32)
    for r in range(rollouts):
        lengths = jnp.where(lane == r, suffix_len[r], lengths)
        current = jnp.where(lane == r, leaf[r], current)
    limits = [jnp.zeros((1, rows), jnp.int32) for _ in range(node_count)]
    for _ in range(node_count):
        lifted = jnp.full((1, rows), -1, jnp.int32)
        for node in range(node_count):
            hit = current == node
            limits[node] = jnp.where(hit, node_len[node], limits[node])
            lifted = jnp.where(hit, parent[node], lifted)
        current = lifted
    first = lane * suf
    last = first + lengths

    def stack(block):
        return [block[:, j * HEAD_DIM:(j + 1) * HEAD_DIM] for j in range(GROUP)]

    def ranked(k):
        near = jnp.minimum(c, n - 1 - c)
        by_two = c - (k + 1) // 2 if k % 2 else c + (k + 1) // 2
        single = jnp.where(2 * c > n - 1, c - (k - near), c + (k - near))
        return jnp.where(k <= 2 * near, by_two, single)

    def pump(d, g):
        @pl.when(c - d >= 0)
        def _():
            pass_copy(0, c - d, c - d, g).wait_recv()

            @pl.when(c + 1 < n)
            def _():
                pass_copy(0, c - d, c + 1, g).start()

        @pl.when(c + d < n)
        def _():
            pass_copy(1, c + d, c + d, g).wait_recv()

            @pl.when(c >= 1)
            def _():
                pass_copy(1, c + d, c - 1, g).start()

    def send(dest, g, mixed, stat):
        o_out[dest, g] = mixed.astype(jnp.bfloat16)
        l_out[dest, g] = stat

        @pl.when(dest < c)
        def _():
            for copy in result_copies(dest, 0, c - 1, g):
                copy.start()

        @pl.when(dest > c)
        def _():
            for copy in result_copies(dest, 1, c + 1, g):
                copy.start()

    def emit(dest, g, mixed, stat):
        edge = ((dest < c) & (c == n - 1)) | ((dest > c) & (c == 0))

        @pl.when(edge)
        def _():
            send(dest, g, mixed, stat)

        @pl.when(jnp.logical_not(edge))
        def _():
            o_part[dest, g] = mixed
            l_part[dest, g] = stat

    def pair_item(pair, g):
        one, two = (ranked(2 * pair) if pair else c), ranked(2 * pair + 1)
        query = jnp.concatenate(stack(qg[one, :, cols(g)]) + stack(qg[two, :, cols(g)]), axis=0)
        if pair == 0:
            vt[g] = prefix[1, :, head_cols(g)].T
        scores = dot_t(prefix[0, :, head_cols(g)], query)
        peak = jnp.max(scores, axis=0, keepdims=True) * COEF
        weights = jnp.exp2(scores * COEF - peak)
        total = jnp.sum(weights, axis=0, keepdims=True)
        mixed = jnp.dot(vt[g], weights.astype(jnp.bfloat16), preferred_element_type=jnp.float32)
        mixed = mixed * (1.0 / total)
        stat = peak + jnp.log2(total)
        if pair:
            emit(one, g, mixed[:, :rows], stat[:, :rows])
        else:
            o_loc[0, g] = mixed[:, :rows]
            l_loc[0, g] = stat[:, :rows]
        emit(two, g, mixed[:, rows:], stat[:, rows:])

    def merge(dest, side, g):
        for copy in result_copies(dest, side, dest, g):
            copy.wait_recv()
        stat_a, stat_b = l_part[dest, g], l_in[side, dest, g]
        peak = jnp.maximum(stat_a, stat_b)
        share_a, share_b = jnp.exp2(stat_a - peak), jnp.exp2(stat_b - peak)
        total = share_a + share_b
        scale = 1.0 / total
        mixed = o_part[dest, g] * (share_a * scale) + o_in[side, dest, g].astype(jnp.float32) * (share_b * scale)
        send(dest, g, mixed, peak + jnp.log2(total))

    def local_item(g):
        query = jnp.concatenate(stack(qg[c, :, cols(g)]), axis=0)
        pieces = []
        keys = suffix[0, :, :, head_cols(g)].reshape(rollouts * suf, HEAD_DIM)
        token = lax.broadcasted_iota(jnp.int32, (rollouts * suf, rows), 0)
        scores = jnp.where((token >= first) & (token < last), dot_t(keys, query), -jnp.inf)
        pieces.append((scores, suffix[1, :, :, head_cols(g)].reshape(rollouts * suf, HEAD_DIM)))
        spot = lax.broadcasted_iota(jnp.int32, (NODE_LEN, rows), 0)
        for node in range(node_count):
            owner, inner = node // nodes.shape[2], node % nodes.shape[2]
            scores = dot_t(nodes[owner, 0, inner, :, head_cols(g)], query)
            scores = jnp.where(spot < limits[node], scores, -jnp.inf)
            pieces.append((scores, nodes[owner, 1, inner, :, head_cols(g)]))
        spot = lax.broadcasted_iota(jnp.int32, (rollouts, rows), 0)
        scores = jnp.where(spot == lane, dot_t(new_ref[0, :, head_cols(g)], query), -jnp.inf)
        pieces.append((scores, new_ref[1, :, head_cols(g)]))
        peak = functools.reduce(jnp.maximum, [jnp.max(s, axis=0, keepdims=True) for s, _ in pieces]) * COEF
        total, mixed = 0.0, 0.0
        for scores, values in pieces:
            weights = jnp.exp2(scores * COEF - peak)
            total = total + jnp.sum(weights, axis=0, keepdims=True)
            mixed = mixed + lax.dot_general(
                values, weights.astype(jnp.bfloat16), (((0,), (0,)), ((), ())),
                preferred_element_type=jnp.float32)
        return mixed / total, peak + jnp.log2(total)

    loads[0].wait()
    loads[1].wait()
    tail = KV_HEADS * (n // 2 - 1)

    @pl.loop(0, tail + max(2 * KV_HEADS, KV_HEADS + LAG * (n - 2)))
    def _(time):
        t = time - tail
        for d in range(1, n):
            ahead = time - STEP * (d - 1)

            @pl.when((ahead >= 0) & (ahead < KV_HEADS))
            def _():
                pump(d, ahead)

        for pair in range(n // 2):
            turn = time - KV_HEADS * pair

            @pl.when((turn >= 0) & (turn < KV_HEADS))
            def _():
                pair_item(pair, turn)

        for ring in range(1, n - 1):
            g = t - LAG * ring

            @pl.when((g >= 0) & (g < KV_HEADS))
            def _():
                @pl.when(c == n - 1 - ring)
                def _():
                    for dest in range(n - 1 - ring):
                        merge(dest, 0, g)

                @pl.when(c == ring)
                def _():
                    for dest in range(ring + 1, n):
                        merge(dest, 1, g)

        @pl.when(t == KV_HEADS - 2)
        def _():
            for k in range(1, chips):
                slot = lax.rem(b + 2 * k, nb)
                node_pass(slot, n_pass.at[k]).wait_recv()
                node_pass(slot, n_pass.at[k]).start()

        @pl.when(t == KV_HEADS)
        def _():
            for load in loads[2:5]:
                load.wait()
            for k in range(chips):
                slot = lax.rem(twin + 2 * k, nb)
                node_pass(slot, n_pass.at[k]).wait_recv()

        @pl.when((t >= KV_HEADS) & (t < 2 * KV_HEADS))
        def _():
            g = t - KV_HEADS
            mixed, stat = local_item(g)
            o_loc[1, g] = mixed
            l_loc[1, g] = stat

    @pl.loop(0, KV_HEADS)
    def _(g):
        for side, alone in ((0, c == n - 1), (1, c == 0)):
            @pl.when(alone)
            def _():
                o_in[side, c, g] = jnp.zeros((HEAD_DIM, rows), jnp.bfloat16)
                l_in[side, c, g] = jnp.full((1, rows), -jnp.inf, jnp.float32)

            @pl.when(jnp.logical_not(alone))
            def _():
                for copy in result_copies(c, side, c, g):
                    copy.wait_recv()

        stats = [l_loc[0, g], l_loc[1, g], l_in[0, c, g], l_in[1, c, g]]
        parts = [o_loc[0, g], o_loc[1, g], o_in[0, c, g], o_in[1, c, g]]
        peak = functools.reduce(jnp.maximum, stats)
        shares = [jnp.exp2(stat - peak) for stat in stats]
        scale = 1.0 / functools.reduce(jnp.add, shares)
        mixed = functools.reduce(
            jnp.add, [part.astype(jnp.float32) * (share * scale) for part, share in zip(parts, shares)])
        done = mixed.T.astype(jnp.bfloat16)
        for j in range(GROUP):
            out_ref[:, pl.ds(pl.multiple_of(g * GW + j * HEAD_DIM, HEAD_DIM), HEAD_DIM)] = (
                done[j * rollouts:(j + 1) * rollouts])

    @pl.loop(0, KV_HEADS)
    def _(g):
        @pl.when(c + 1 < n)
        def _():
            own_copy(0, c + 1, g).wait_send()

        @pl.when(c >= 1)
        def _():
            own_copy(1, c - 1, g).wait_send()

        for d in range(1, n):
            @pl.when((c - d >= 0) & (c + 1 < n))
            def _():
                pass_copy(0, c - d, c + 1, g).wait_send()

            @pl.when((c + d < n) & (c >= 1))
            def _():
                pass_copy(1, c + d, c - 1, g).wait_send()

            for copy in result_copies(lax.rem(c + d, n), 0, lax.rem(c + d, n), g):
                copy.wait_send()

    for k in range(1, chips):
        node_copy(lax.rem(b + 2 * k, nb), b, n_send.at[k]).wait_send()
        node_pass(lax.rem(b + 2 * k, nb), n_pass.at[k]).wait_send()
    node_copy(twin, b, n_send.at[0]).wait_send()


def on_device(n, nb, prefix_kv, queries, new_kv, suffix_kv, suffix_len, node_kv, node_len, parent, leaf):
    rows = queries.shape[0] * GROUP
    dma = pltpu.SemaphoreType.DMA
    bf16, f32 = jnp.bfloat16, jnp.float32
    return pl.pallas_call(
        functools.partial(kernel, n, nb),
        out_shape=jax.ShapeDtypeStruct(queries.shape, bf16),
        in_specs=[pl.BlockSpec(memory_space=pltpu.HBM)] * 9,
        out_specs=pl.BlockSpec(memory_space=pltpu.VMEM),
        scratch_shapes=[
            pltpu.SMEM(suffix_len.shape, jnp.int32),
            pltpu.SMEM(node_len.shape, jnp.int32),
            pltpu.SMEM(parent.shape, jnp.int32),
            pltpu.SMEM(leaf.shape, jnp.int32),
            pltpu.VMEM(new_kv.shape, bf16),
            pltpu.VMEM(prefix_kv.shape, bf16),
            pltpu.VMEM(suffix_kv.shape, bf16),
            pltpu.VMEM((nb,) + node_kv.shape, bf16),
            pltpu.VMEM((KV_HEADS, HEAD_DIM, prefix_kv.shape[1]), bf16),
            pltpu.VMEM((n,) + queries.shape, bf16),
            pltpu.VMEM((n, KV_HEADS, HEAD_DIM, rows), f32),
            pltpu.VMEM((n, KV_HEADS, 1, rows), f32),
            pltpu.VMEM((n, KV_HEADS, HEAD_DIM, rows), bf16),
            pltpu.VMEM((n, KV_HEADS, 1, rows), f32),
            pltpu.VMEM((2, n, KV_HEADS, HEAD_DIM, rows), bf16),
            pltpu.VMEM((2, n, KV_HEADS, 1, rows), f32),
            pltpu.VMEM((2, KV_HEADS, HEAD_DIM, rows), f32),
            pltpu.VMEM((2, KV_HEADS, 1, rows), f32),
            dma((9,)),
            dma((2, n, KV_HEADS)),
            dma((n, KV_HEADS)),
            dma((n, KV_HEADS)),
            dma((2, n, KV_HEADS)),
            dma((n, KV_HEADS)),
            dma((2, n, KV_HEADS)),
            dma((nb // 2,)),
            dma((nb // 2,)),
            dma((nb,)),
        ],
        compiler_params=pltpu.CompilerParams(
            collective_id=0, has_side_effects=True, vmem_limit_bytes=63 * 1024 * 1024),
    )(suffix_len, node_len, parent, leaf, queries, new_kv, prefix_kv, suffix_kv, node_kv)


def solution(mesh):
    return jax.shard_map(
        functools.partial(on_device, mesh.shape["ctx"], mesh.shape["branch"]),
        mesh=mesh,
        in_specs=(
            P(None, ("parts", "ctx"), None),
            P(("parts", "ctx", "branch"), None),
            P(None, ("parts", "ctx", "branch"), None),
            P(None, ("parts", "ctx", "branch"), None, None),
            P(("parts", "ctx", "branch")),
            P(None, ("parts", "branch"), None, None),
            P("parts"),
            P("parts"),
            P(("parts", "ctx", "branch")),
        ),
        out_specs=P(("parts", "ctx", "branch"), None),
        check_vma=False,
    )
```

```python
import functools
import math

import jax
import jax.numpy as jnp
from jax import lax
from jax.experimental import pallas as pl
from jax.experimental.pallas import tpu as pltpu
from jax.sharding import PartitionSpec as P

HEADS = 64
KV_HEADS = 8
HEAD_DIM = 128
NODE_LEN = 128
GROUP = HEADS // KV_HEADS
GW = GROUP * HEAD_DIM
MESH = pl.DeviceIdType.MESH
LOG2E = math.log2(math.e)
COEF = HEAD_DIM ** (-0.5) * LOG2E


def dot_t(keys, rows):
    return lax.dot_general(keys, rows, (((1,), (1,)), ((), ())), preferred_element_type=jnp.float32)
LAG = 4
STEP = 4


def kernel(
    n, nb, suffix_len_hbm, node_len_hbm, parent_hbm, leaf_hbm, q_hbm, new_hbm, prefix_hbm, suffix_hbm, node_hbm,
    out_ref,
    suffix_len, node_len, parent, leaf, new_ref, prefix, suffix, nodes, vt, qg,
    o_part, l_part, o_out, l_out, o_in, l_in, o_loc, l_loc,
    load_sem, q_send, q_recv, r_send, r_recv, l_send, l_recv, n_send, n_pass, n_recv,
):
    c = lax.axis_index("ctx")
    b = lax.axis_index("branch")
    rollouts = qg.shape[1]
    rows = rollouts * GROUP
    node_count = node_len.shape[0]
    suf = suffix.shape[2]
    chips = nb // 2
    core = lax.rem(b, 2)
    twin = b + 1 - 2 * core

    barrier = pltpu.get_barrier_semaphore()
    @pl.when(c + 1 < n)
    def _():
        pl.semaphore_signal(barrier, inc=1, device_id={"ctx": c + 1}, device_id_type=MESH)

    @pl.when(c >= 1)
    def _():
        pl.semaphore_signal(barrier, inc=1, device_id={"ctx": c - 1}, device_id_type=MESH)

    pl.semaphore_signal(barrier, inc=1, device_id={"branch": twin}, device_id_type=MESH)
    for k in range(1, chips):
        pl.semaphore_signal(barrier, inc=1, device_id={"branch": lax.rem(b + 2 * k, nb)}, device_id_type=MESH)

    loads = [
        pltpu.make_async_copy(src, dst, load_sem.at[i])
        for i, (src, dst) in enumerate([
            (q_hbm, qg.at[c]), (prefix_hbm, prefix), (suffix_hbm, suffix), (node_hbm, nodes.at[b]),
            (new_hbm, new_ref), (suffix_len_hbm, suffix_len), (node_len_hbm, node_len),
            (parent_hbm, parent), (leaf_hbm, leaf)])
    ]
    for load in loads:
        load.start()

    @pl.when((c >= 1) & (c + 1 < n))
    def _():
        pl.semaphore_wait(barrier, chips + 2)

    @pl.when((c == 0) | (c == n - 1))
    def _():
        pl.semaphore_wait(barrier, chips + 1)

    def cols(g):
        return pl.ds(pl.multiple_of(g * GW, GW), GW)

    def head_cols(g):
        return pl.ds(pl.multiple_of(g * HEAD_DIM, HEAD_DIM), HEAD_DIM)

    def own_copy(side, target, g):
        return pltpu.make_async_remote_copy(
            src_ref=q_hbm.at[:, cols(g)], dst_ref=qg.at[c, :, cols(g)],
            send_sem=q_send.at[side, c, g], recv_sem=q_recv.at[c, g],
            device_id={"ctx": target}, device_id_type=MESH)

    def pass_copy(side, src, target, g):
        return pltpu.make_async_remote_copy(
            src_ref=qg.at[src, :, cols(g)], dst_ref=qg.at[src, :, cols(g)],
            send_sem=q_send.at[side, src, g], recv_sem=q_recv.at[src, g],
            device_id={"ctx": target}, device_id_type=MESH)

    def result_copies(dest, side, target, g):
        return (
            pltpu.make_async_remote_copy(
                src_ref=o_out.at[dest, g], dst_ref=o_in.at[side, dest, g],
                send_sem=r_send.at[dest, g], recv_sem=r_recv.at[side, dest, g],
                device_id={"ctx": target}, device_id_type=MESH),
            pltpu.make_async_remote_copy(
                src_ref=l_out.at[dest, g], dst_ref=l_in.at[side, dest, g],
                send_sem=l_send.at[dest, g], recv_sem=l_recv.at[side, dest, g],
                device_id={"ctx": target}, device_id_type=MESH))

    def node_copy(peer, slot, sem):
        return pltpu.make_async_remote_copy(
            src_ref=node_hbm, dst_ref=nodes.at[slot], send_sem=sem, recv_sem=n_recv.at[slot],
            device_id={"branch": peer}, device_id_type=MESH)

    def node_pass(slot, sem):
        return pltpu.make_async_remote_copy(
            src_ref=nodes.at[slot], dst_ref=nodes.at[slot], send_sem=sem, recv_sem=n_recv.at[slot],
            device_id={"branch": twin}, device_id_type=MESH)

    @pl.loop(0, KV_HEADS)
    def _(g):
        @pl.when(c + 1 < n)
        def _():
            own_copy(0, c + 1, g).start()

        @pl.when(c >= 1)
        def _():
            own_copy(1, c - 1, g).start()

    for k in range(1, chips):
        node_copy(lax.rem(b + 2 * k, nb), b, n_send.at[k]).start()
    node_copy(twin, b, n_send.at[0]).start()

    for load in loads[5:]:
        load.wait()
    lane = lax.rem(lax.broadcasted_iota(jnp.int32, (1, rows), 1), rollouts)
    lengths = jnp.zeros((1, rows), jnp.int32)
    current = jnp.zeros((1, rows), jnp.int32)
    for r in range(rollouts):
        lengths = jnp.where(lane == r, suffix_len[r], lengths)
        current = jnp.where(lane == r, leaf[r], current)
    limits = [jnp.zeros((1, rows), jnp.int32) for _ in range(node_count)]
    for _ in range(node_count):
        lifted = jnp.full((1, rows), -1, jnp.int32)
        for node in range(node_count):
            hit = current == node
            limits[node] = jnp.where(hit, node_len[node], limits[node])
            lifted = jnp.where(hit, parent[node], lifted)
        current = lifted
    first = lane * suf
    last = first + lengths

    def stack(block):
        return [block[:, j * HEAD_DIM:(j + 1) * HEAD_DIM] for j in range(GROUP)]

    def ranked(k):
        near = jnp.minimum(c, n - 1 - c)
        by_two = c - (k + 1) // 2 if k % 2 else c + (k + 1) // 2
        single = jnp.where(2 * c > n - 1, c - (k - near), c + (k - near))
        return jnp.where(k <= 2 * near, by_two, single)

    def pump(d, g):
        @pl.when(c - d >= 0)
        def _():
            pass_copy(0, c - d, c - d, g).wait_recv()

            @pl.when(c + 1 < n)
            def _():
                pass_copy(0, c - d, c + 1, g).start()

        @pl.when(c + d < n)
        def _():
            pass_copy(1, c + d, c + d, g).wait_recv()

            @pl.when(c >= 1)
            def _():
                pass_copy(1, c + d, c - 1, g).start()

    def send(dest, g, mixed, stat):
        o_out[dest, g] = mixed.astype(jnp.bfloat16)
        l_out[dest, g] = stat

        @pl.when(dest < c)
        def _():
            for copy in result_copies(dest, 0, c - 1, g):
                copy.start()

        @pl.when(dest > c)
        def _():
            for copy in result_copies(dest, 1, c + 1, g):
                copy.start()

    def emit(dest, g, mixed, stat):
        edge = ((dest < c) & (c == n - 1)) | ((dest > c) & (c == 0))

        @pl.when(edge)
        def _():
            send(dest, g, mixed, stat)

        @pl.when(jnp.logical_not(edge))
        def _():
            o_part[dest, g] = mixed
            l_part[dest, g] = stat

    def pair_item(pair, g):
        one, two = (ranked(2 * pair) if pair else c), ranked(2 * pair + 1)
        query = jnp.concatenate(stack(qg[one, :, cols(g)]) + stack(qg[two, :, cols(g)]), axis=0)
        if pair == 0:
            vt[g] = prefix[1, :, head_cols(g)].T
        scores = dot_t(prefix[0, :, head_cols(g)], query)
        peak = jnp.max(scores, axis=0, keepdims=True) * COEF
        weights = jnp.exp2(scores * COEF - peak)
        total = jnp.sum(weights, axis=0, keepdims=True)
        mixed = jnp.dot(vt[g], weights.astype(jnp.bfloat16), preferred_element_type=jnp.float32)
        mixed = mixed * (1.0 / total)
        stat = peak + jnp.log2(total)
        emit(two, g, mixed[:, rows:], stat[:, rows:])
        if pair:
            emit(one, g, mixed[:, :rows], stat[:, :rows])
        else:
            o_loc[0, g] = mixed[:, :rows]
            l_loc[0, g] = stat[:, :rows]

    def merge(dest, side, g):
        for copy in result_copies(dest, side, dest, g):
            copy.wait_recv()
        stat_a, stat_b = l_part[dest, g], l_in[side, dest, g]
        peak = jnp.maximum(stat_a, stat_b)
        share_a, share_b = jnp.exp2(stat_a - peak), jnp.exp2(stat_b - peak)
        total = share_a + share_b
        scale = 1.0 / total
        mixed = o_part[dest, g] * (share_a * scale) + o_in[side, dest, g].astype(jnp.float32) * (share_b * scale)
        send(dest, g, mixed, peak + jnp.log2(total))

    def local_item(g):
        query = jnp.concatenate(stack(qg[c, :, cols(g)]), axis=0)
        pieces = []
        keys = suffix[0, :, :, head_cols(g)].reshape(rollouts * suf, HEAD_DIM)
        token = lax.broadcasted_iota(jnp.int32, (rollouts * suf, rows), 0)
        scores = jnp.where((token >= first) & (token < last), dot_t(keys, query), -jnp.inf)
        pieces.append((scores, suffix[1, :, :, head_cols(g)].reshape(rollouts * suf, HEAD_DIM)))
        spot = lax.broadcasted_iota(jnp.int32, (NODE_LEN, rows), 0)
        for node in range(node_count):
            owner, inner = node // nodes.shape[2], node % nodes.shape[2]
            scores = dot_t(nodes[owner, 0, inner, :, head_cols(g)], query)
            scores = jnp.where(spot < limits[node], scores, -jnp.inf)
            pieces.append((scores, nodes[owner, 1, inner, :, head_cols(g)]))
        spot = lax.broadcasted_iota(jnp.int32, (rollouts, rows), 0)
        scores = jnp.where(spot == lane, dot_t(new_ref[0, :, head_cols(g)], query), -jnp.inf)
        pieces.append((scores, new_ref[1, :, head_cols(g)]))
        peak = functools.reduce(jnp.maximum, [jnp.max(s, axis=0, keepdims=True) for s, _ in pieces]) * COEF
        total, mixed = 0.0, 0.0
        for scores, values in pieces:
            weights = jnp.exp2(scores * COEF - peak)
            total = total + jnp.sum(weights, axis=0, keepdims=True)
            mixed = mixed + lax.dot_general(
                values, weights.astype(jnp.bfloat16), (((0,), (0,)), ((), ())),
                preferred_element_type=jnp.float32)
        return mixed / total, peak + jnp.log2(total)

    loads[0].wait()
    loads[1].wait()
    tail = KV_HEADS * (n // 2 - 1)

    @pl.loop(0, tail + max(2 * KV_HEADS, KV_HEADS + LAG * (n - 2)))
    def _(time):
        t = time - tail
        for d in range(1, n):
            ahead = time - STEP * (d - 1)

            @pl.when((ahead >= 0) & (ahead < KV_HEADS))
            def _():
                pump(d, ahead)

        for pair in range(n // 2):
            turn = time - KV_HEADS * pair

            @pl.when((turn >= 0) & (turn < KV_HEADS))
            def _():
                pair_item(pair, turn)

        for ring in range(1, n - 1):
            g = t - LAG * ring

            @pl.when((g >= 0) & (g < KV_HEADS))
            def _():
                @pl.when(c == n - 1 - ring)
                def _():
                    for dest in range(n - 1 - ring):
                        merge(dest, 0, g)

                @pl.when(c == ring)
                def _():
                    for dest in range(n - 1, ring, -1):
                        merge(dest, 1, g)

        @pl.when(t == KV_HEADS - 2)
        def _():
            for k in range(1, chips):
                slot = lax.rem(b + 2 * k, nb)
                node_pass(slot, n_pass.at[k]).wait_recv()
                node_pass(slot, n_pass.at[k]).start()

        @pl.when(t == KV_HEADS)
        def _():
            for load in loads[2:5]:
                load.wait()
            for k in range(chips):
                slot = lax.rem(twin + 2 * k, nb)
                node_pass(slot, n_pass.at[k]).wait_recv()

        @pl.when((t >= KV_HEADS) & (t < 2 * KV_HEADS))
        def _():
            g = t - KV_HEADS
            mixed, stat = local_item(g)
            o_loc[1, g] = mixed
            l_loc[1, g] = stat

    @pl.loop(0, KV_HEADS)
    def _(g):
        for side, alone in ((0, c == n - 1), (1, c == 0)):
            @pl.when(alone)
            def _():
                o_in[side, c, g] = jnp.zeros((HEAD_DIM, rows), jnp.bfloat16)
                l_in[side, c, g] = jnp.full((1, rows), -jnp.inf, jnp.float32)

            @pl.when(jnp.logical_not(alone))
            def _():
                for copy in result_copies(c, side, c, g):
                    copy.wait_recv()

        stats = [l_loc[0, g], l_loc[1, g], l_in[0, c, g], l_in[1, c, g]]
        parts = [o_loc[0, g], o_loc[1, g], o_in[0, c, g], o_in[1, c, g]]
        peak = functools.reduce(jnp.maximum, stats)
        shares = [jnp.exp2(stat - peak) for stat in stats]
        scale = 1.0 / functools.reduce(jnp.add, shares)
        mixed = functools.reduce(
            jnp.add, [part.astype(jnp.float32) * (share * scale) for part, share in zip(parts, shares)])
        done = mixed.T.astype(jnp.bfloat16)
        for j in range(GROUP):
            out_ref[:, pl.ds(pl.multiple_of(g * GW + j * HEAD_DIM, HEAD_DIM), HEAD_DIM)] = (
                done[j * rollouts:(j + 1) * rollouts])

    @pl.loop(0, KV_HEADS)
    def _(g):
        @pl.when(c + 1 < n)
        def _():
            own_copy(0, c + 1, g).wait_send()

        @pl.when(c >= 1)
        def _():
            own_copy(1, c - 1, g).wait_send()

        for d in range(1, n):
            @pl.when((c - d >= 0) & (c + 1 < n))
            def _():
                pass_copy(0, c - d, c + 1, g).wait_send()

            @pl.when((c + d < n) & (c >= 1))
            def _():
                pass_copy(1, c + d, c - 1, g).wait_send()

            for copy in result_copies(lax.rem(c + d, n), 0, lax.rem(c + d, n), g):
                copy.wait_send()

    for k in range(1, chips):
        node_copy(lax.rem(b + 2 * k, nb), b, n_send.at[k]).wait_send()
        node_pass(lax.rem(b + 2 * k, nb), n_pass.at[k]).wait_send()
    node_copy(twin, b, n_send.at[0]).wait_send()


def on_device(n, nb, prefix_kv, queries, new_kv, suffix_kv, suffix_len, node_kv, node_len, parent, leaf):
    rows = queries.shape[0] * GROUP
    dma = pltpu.SemaphoreType.DMA
    bf16, f32 = jnp.bfloat16, jnp.float32
    return pl.pallas_call(
        functools.partial(kernel, n, nb),
        out_shape=jax.ShapeDtypeStruct(queries.shape, bf16),
        in_specs=[pl.BlockSpec(memory_space=pltpu.HBM)] * 9,
        out_specs=pl.BlockSpec(memory_space=pltpu.VMEM),
        scratch_shapes=[
            pltpu.SMEM(suffix_len.shape, jnp.int32),
            pltpu.SMEM(node_len.shape, jnp.int32),
            pltpu.SMEM(parent.shape, jnp.int32),
            pltpu.SMEM(leaf.shape, jnp.int32),
            pltpu.VMEM(new_kv.shape, bf16),
            pltpu.VMEM(prefix_kv.shape, bf16),
            pltpu.VMEM(suffix_kv.shape, bf16),
            pltpu.VMEM((nb,) + node_kv.shape, bf16),
            pltpu.VMEM((KV_HEADS, HEAD_DIM, prefix_kv.shape[1]), bf16),
            pltpu.VMEM((n,) + queries.shape, bf16),
            pltpu.VMEM((n, KV_HEADS, HEAD_DIM, rows), f32),
            pltpu.VMEM((n, KV_HEADS, 1, rows), f32),
            pltpu.VMEM((n, KV_HEADS, HEAD_DIM, rows), bf16),
            pltpu.VMEM((n, KV_HEADS, 1, rows), f32),
            pltpu.VMEM((2, n, KV_HEADS, HEAD_DIM, rows), bf16),
            pltpu.VMEM((2, n, KV_HEADS, 1, rows), f32),
            pltpu.VMEM((2, KV_HEADS, HEAD_DIM, rows), f32),
            pltpu.VMEM((2, KV_HEADS, 1, rows), f32),
            dma((9,)),
            dma((2, n, KV_HEADS)),
            dma((n, KV_HEADS)),
            dma((n, KV_HEADS)),
            dma((2, n, KV_HEADS)),
            dma((n, KV_HEADS)),
            dma((2, n, KV_HEADS)),
            dma((nb // 2,)),
            dma((nb // 2,)),
            dma((nb,)),
        ],
        compiler_params=pltpu.CompilerParams(
            collective_id=0, has_side_effects=True, vmem_limit_bytes=63 * 1024 * 1024),
    )(suffix_len, node_len, parent, leaf, queries, new_kv, prefix_kv, suffix_kv, node_kv)


def solution(mesh):
    return jax.shard_map(
        functools.partial(on_device, mesh.shape["ctx"], mesh.shape["branch"]),
        mesh=mesh,
        in_specs=(
            P(None, ("parts", "ctx"), None),
            P(("parts", "ctx", "branch"), None),
            P(None, ("parts", "ctx", "branch"), None),
            P(None, ("parts", "ctx", "branch"), None, None),
            P(("parts", "ctx", "branch")),
            P(None, ("parts", "branch"), None, None),
            P("parts"),
            P("parts"),
            P(("parts", "ctx", "branch")),
        ),
        out_specs=P(("parts", "ctx", "branch"), None),
        check_vma=False,
    )
```
